512 devices in a mesh: dp: 2 (over core), expert: 32 (over y, x), tensor: 8 (over z).
Axes of the slice: x: 4, y: 8, z: 8, core: 2. Of those that a mesh axis runs over, the one named last changes fastest.
Arguments:
- tokens: bfloat16 [4096, 2048], P(('dp', 'expert'), 'tensor'), may hold values from -6 to 6
- expert_ids: int32 [4096, 6], P(('dp', 'expert')), may hold values from 0 to 31, all different within a row; in each aligned block of 64 rows (0 to 63, 64 to 127, ...) at most 16 rows name the same one
- route_weights: float32 [4096, 6], P(('dp', 'expert')), may hold values from 0.1 to 1
- w_gate: bfloat16 [32, 1408, 2048], P('expert', 'tensor'), may hold values from -0.125 to 0.125
- w_up: bfloat16 [32, 1408, 2048], P('expert', 'tensor'), may hold values from -0.125 to 0.125
- w_down: bfloat16 [32, 1408, 2048], P('expert', 'tensor'), may hold values from -0.15625 to 0.15625
- out_grad: bfloat16 [4096, 2048], P(('dp', 'expert'), 'tensor'), may hold values from -6 to 6
Outputs:
- layer_out: bfloat16 [4096, 2048], P(('dp', 'expert'), 'tensor')
- grad_tokens: bfloat16 [4096, 2048], P(('dp', 'expert'), 'tensor')
- grad_weights: float32 [4096, 6], P(('dp', 'expert'))
- grad_gate: bfloat16 [32, 1408, 2048], P('expert', 'tensor')
- grad_up: bfloat16 [32, 1408, 2048], P('expert', 'tensor')
- grad_down: bfloat16 [32, 1408, 2048], P('expert', 'tensor')
The draws below stay inside these ranges and needn't reach their ends.
Inputs may be any that keep to these rules, and one draw needn't show every extreme that they name: `expert_ids`: each row names 6 different experts. In each aligned block of 64 rows no expert is named more than 16 times, a bound that some block reaches.
All inputs are finite; a program needn't handle non-finite values.
Results may differ from the reference program's by a relative error of at most 0.014.
Values may be sent and summed in bfloat16 or wider, within the bound.
No kernel may reach another device: no remote copies, remote signals or barrier semaphores. Data moves between devices by JAX's collectives and lax.ppermute only.
A program may use at most 128 MiB of HBM per device.

```python
import math
import jax
import jax.numpy as jnp
import numpy as np
from jax import lax

D = 2048
H = 1408
TOPK = 6
TOK_DEV = 64
EXPERTS = 32
CAP = 16
TOKENS = 4096
N_DP = 2
N_EXPERT = 32
N_TENSOR = 8


def block_levels(key, extent, pieces, smallest, high):
    level = 1.0
    for dim, blocks in pieces:
        steps = jax.random.uniform(jax.random.fold_in(jax.random.fold_in(key, 6), dim), (blocks,), jnp.float32, smallest / len(pieces), high / len(pieces))
        level = level * jnp.repeat(jnp.exp(steps), extent[dim] // blocks).reshape((-1,) + (1,) * (len(extent) - 1 - dim))
    return level


def deal_out(key, own, number, rows, count, top, reach, skew):
    ranking = jax.random.permutation(key, count)
    packed, ordinary = portions_of(count, rows * top, reach, skew, True), portions_of(count, rows * top, reach, skew, False)
    places = jnp.arange(count)

    def named(tallies, rotation):
        used = int((tallies > 0).sum())
        fixed = max(1, used // 4)
        passed = fixed + (places - fixed + rotation * (used - fixed)) % max(1, count - fixed)
        return jnp.zeros((count,), jnp.int32).at[ranking[jnp.where(places < fixed, places, passed)]].set(jnp.asarray(tallies, jnp.int32))

    tallies = jnp.where(number % 4 == 0, named(packed, number // 4), named(ordinary, number - number // 4 - 1))
    mixed = jax.random.permutation(jax.random.fold_in(own, 3), count)
    giver, receiver = mixed[0:count // 2 * 2:2], mixed[1:count // 2 * 2:2]
    room = jnp.minimum(tallies[giver] - 1, reach - tallies[receiver]) // 2
    room = jnp.where((giver == ranking[0]) | (receiver == ranking[0]) | (tallies[receiver] == 0), 0, jnp.maximum(room, 0))
    passed = jax.random.randint(jax.random.fold_in(own, 4), (count // 2,), 0, 1 << 20) % (room + 1)
    tallies = tallies.at[giver].add(-passed).at[receiver].add(passed)
    members = jnp.searchsorted(jnp.cumsum(tallies), jnp.arange(rows * top), side="right").astype(jnp.int32)
    grid = members.reshape(top, rows).T
    grid = grid[jax.random.permutation(jax.random.fold_in(own, 1), rows)]
    rotation = jax.random.randint(jax.random.fold_in(own, 2), (rows, 1), 0, top)
    return jnp.take_along_axis(grid, (jnp.arange(top)[None, :] + rotation) % top, axis=1)


def portions_of(amount, total, limit, skew, full):
    loads = [(1 << 20) // math.isqrt(standing ** skew) + 1 for standing in range(1, amount + 1)]
    largest = limit if full else min(limit, max(-(-total // amount), total * loads[0] // sum(loads)))
    least = 1 if total - largest >= amount - 1 else 0
    counts, rest = [largest] + [least] * (amount - 1), total - largest - least * (amount - 1)
    while rest > 0:
        movable = [i for i in range(1, amount) if counts[i] < largest] or [i for i in range(1, amount) if counts[i] < limit]
        pool, budget = sum([loads[i] for i in movable]), rest
        for i in movable:
            addition = min(limit - counts[i], max(1, budget * loads[i] // pool), rest)
            counts[i] = counts[i] + addition
            rest = rest - addition
    return np.array(counts)


def noise(stream_key, extent, spread, most, cuts=(), held_as=jnp.bfloat16):
    array = spread * jax.random.normal(stream_key, extent, jnp.float32)
    if cuts:
        array = array * block_levels(stream_key, extent, cuts, -0.22, 0.18)
    return jnp.clip(array, -most, most).astype(held_as)


def setup_inputs(seed: int = 0) -> dict:
    seeds = jax.random.split(jax.random.key(seed), 8)
    tokens = noise(seeds[0], (TOKENS, D), 1.0, 6.0, ((0, 64), (1, 8)))
    expert_ids_keys = jax.random.split(jax.random.fold_in(seeds[1], 1), TOKENS // TOK_DEV)
    expert_ids_turns = jax.random.permutation(jax.random.fold_in(seeds[1], 3), TOKENS // TOK_DEV)
    expert_ids = jax.vmap(lambda own, number: deal_out(jax.random.fold_in(seeds[1], 2), own, number, TOK_DEV, EXPERTS, TOPK, CAP, 2))(expert_ids_keys, expert_ids_turns).reshape((TOKENS, TOPK))
    route_weights = jnp.clip(jnp.exp(math.log(1.0) - 2.3025851 * jax.random.uniform(seeds[2], (TOKENS, TOPK), jnp.float32) ** block_levels(seeds[2], (TOKENS, TOPK), ((0, 64),), -0.2, 0.2)), 0.1, 1.0)
    w_gate = noise(seeds[3], (EXPERTS, H, D), D ** -0.5, 0.125, ((0, 32), (1, 8)))
    w_up = noise(seeds[4], (EXPERTS, H, D), D ** -0.5, 0.125, ((0, 32), (1, 8)))
    w_down = noise(seeds[5], (EXPERTS, H, D), H ** -0.5, 0.15625, ((0, 32), (1, 8)))
    out_grad = noise(seeds[6], (TOKENS, D), 1.0, 6.0, ((0, 64), (1, 8)))
    return dict(tokens=tokens, expert_ids=expert_ids, route_weights=route_weights, w_gate=w_gate, w_up=w_up, w_down=w_down, out_grad=out_grad)


def build_slots(block_ids, capacity, experts):
    onehot = (block_ids[:, None] == jnp.arange(experts, dtype=jnp.int32)[None, :]).astype(jnp.int32)
    before = jnp.cumsum(onehot, axis=0) - onehot
    position = jnp.sum(before * onehot, axis=1).astype(jnp.int32)
    slot_index = (block_ids * capacity + position).astype(jnp.int32)
    count = block_ids.shape[0]
    lookup = jnp.full((experts * capacity,), -1, jnp.int32).at[slot_index].set(jnp.arange(count, dtype=jnp.int32))
    return slot_index, lookup


def rounded(value):
    return lax.optimization_barrier(value.astype(jnp.bfloat16)).astype(jnp.float32)


def group_sum(left, right):
    rows = left.shape[0]
    left_groups = left.astype(jnp.float32).reshape(N_DP, rows // N_DP, left.shape[1])
    right_groups = right.astype(jnp.float32).reshape(N_DP, rows // N_DP, right.shape[1])
    terms = jnp.einsum("grd,grh->gdh", left_groups, right_groups)
    return jnp.sum(rounded(terms), axis=0).astype(jnp.bfloat16)


def reference(tokens, expert_ids, route_weights, w_gate, w_up, w_down, out_grad):
    blocks = N_DP * N_EXPERT
    pairs = TOK_DEV * TOPK
    block_width = H // N_TENSOR
    grouped = expert_ids.reshape(blocks, pairs).astype(jnp.int32)
    unused, lookup = jax.vmap(lambda ids: build_slots(ids, CAP, EXPERTS))(grouped)
    base = (jnp.arange(blocks, dtype=jnp.int32) * pairs)[:, None]
    flat_weights = route_weights.reshape(-1)

    def per_expert(carry, expert):
        out_total, grad_total, dot_total = carry
        local = lax.dynamic_slice_in_dim(lookup, expert * CAP, CAP, axis=1)
        filled = (local >= 0).reshape(-1)
        pair_index = jnp.where(local >= 0, local + base, 0).reshape(-1).astype(jnp.int32)
        token_index = (pair_index // TOPK).astype(jnp.int32)
        rows_in = jnp.where(filled[:, None], tokens[token_index], jnp.zeros((), tokens.dtype))
        slot_weight = jnp.where(filled, flat_weights[pair_index], jnp.zeros((), flat_weights.dtype))
        cotangent = out_grad[token_index].astype(jnp.float32)
        scaled = (slot_weight[:, None] * cotangent).astype(jnp.bfloat16)
        gate_matrix = w_gate[expert]
        up_matrix = w_up[expert]
        down_matrix = w_down[expert]
        count = rows_in.shape[0]
        gate_value = jnp.dot(rows_in, gate_matrix.T, preferred_element_type=jnp.float32)
        up_value = jnp.dot(rows_in, up_matrix.T, preferred_element_type=jnp.float32)
        hidden = (jax.nn.silu(gate_value) * up_value).astype(jnp.bfloat16)
        part = jnp.einsum("rbh,bhd->rbd", hidden.astype(jnp.float32).reshape(count, N_TENSOR, block_width),
                          down_matrix.astype(jnp.float32).reshape(N_TENSOR, block_width, D))
        summed = jnp.sum(rounded(part), axis=1)
        out_total = out_total.at[token_index].add(slot_weight[:, None] * summed)
        dots = jnp.where(filled, jnp.sum(cotangent * summed, axis=1), jnp.zeros((), jnp.float32))
        dot_total = dot_total.at[pair_index].add(dots)
        grad_hidden = jnp.dot(scaled, down_matrix.T, preferred_element_type=jnp.float32)
        sigma = jax.nn.sigmoid(gate_value)
        gate_rows = (grad_hidden * up_value * sigma * (1.0 + gate_value * (1.0 - sigma))).astype(jnp.bfloat16)
        up_rows = (grad_hidden * jax.nn.silu(gate_value)).astype(jnp.bfloat16)
        grad_part = jnp.einsum("rbh,bhd->rbd", gate_rows.astype(jnp.float32).reshape(count, N_TENSOR, block_width),
                               gate_matrix.astype(jnp.float32).reshape(N_TENSOR, block_width, D))
        grad_part = grad_part + jnp.einsum("rbh,bhd->rbd", up_rows.astype(jnp.float32).reshape(count, N_TENSOR, block_width),
                                           up_matrix.astype(jnp.float32).reshape(N_TENSOR, block_width, D))
        grad_total = grad_total.at[token_index].add(jnp.sum(rounded(grad_part), axis=1))
        gate_grad = group_sum(gate_rows, rows_in)
        up_grad = group_sum(up_rows, rows_in)
        down_grad = group_sum(hidden, scaled)
        return (out_total, grad_total, dot_total), (gate_grad, up_grad, down_grad)

    start = (jnp.zeros((TOKENS, D), jnp.float32), jnp.zeros((TOKENS, D), jnp.float32),
             jnp.zeros((TOKENS * TOPK,), jnp.float32))
    final, grads = lax.scan(per_expert, start, jnp.arange(EXPERTS, dtype=jnp.int32))
    out_total, grad_total, dot_total = final
    return (out_total.astype(jnp.bfloat16), grad_total.astype(jnp.bfloat16),
            dot_total.reshape(TOKENS, TOPK), grads[0], grads[1], grads[2])
```

```python
import jax
import jax.numpy as jnp
from jax import lax
from jax.experimental import pallas as pl
from jax.experimental.pallas import tpu as pltpu
from jax.sharding import PartitionSpec as P

BF = jnp.bfloat16
F32 = jnp.float32
N_T = 8


def nt(left, right):
    return lax.dot_general(left, right, (((1,), (1,)), ((), ())), preferred_element_type=F32)


def tn(left, right):
    return lax.dot_general(left, right, (((0,), (0,)), ((), ())), preferred_element_type=F32)


def nn(left, right):
    return lax.dot_general(left, right, (((1,), (0,)), ((), ())), preferred_element_type=F32)


def shift(x, by):
    return lax.ppermute(x, "tensor", [(i, (i + by) % N_T) for i in range(N_T)])


def gather_ring(x, g):
    xs, gs = [x] + [None] * (N_T - 1), [g] + [None] * (N_T - 1)
    half = N_T // 2
    for s in range(1, half + 1):
        xs[-s] = shift(xs[(1 - s) % N_T], 1)
        gs[-s if s < half else s] = shift(gs[(1 - s) % N_T], 1) if s < half else shift(gs[s - 1], -1)
        if s < half:
            xs[s] = shift(xs[s - 1], -1)
            gs[s] = shift(gs[s - 1], -1)
    return xs, gs


def reduce_ring(terms, up, down):
    u, d = terms[up], terms[-down % N_T]
    for s in range(1, max(up, down) + 1):
        if s <= up:
            u = shift(u, 1)
            if s < up:
                u = (u.astype(F32) + terms[up - s].astype(F32)).astype(BF)
        if s <= down:
            d = shift(d, -1)
            if s < down:
                d = (d.astype(F32) + terms[(s - down) % N_T].astype(F32)).astype(BF)
    return (terms[0].astype(F32) + u.astype(F32) + d.astype(F32)).astype(BF)


def expert_kernel(meta, *refs):
    xs, gs = refs[:N_T], refs[N_T : 2 * N_T]
    wg, wu, wd, part, gpart, gout, uout, dout = refs[2 * N_T :]
    z = meta[0]
    rows, width = xs[0].shape

    def col(places):
        at = (z + places) & (N_T - 1)
        return pl.ds(pl.multiple_of(at * width, width), width)

    gate_value = nt(xs[0][...], wg[:, col(0)])
    up_value = nt(xs[0][...], wu[:, col(0)])
    grad_hidden = nt(gs[0][...], wd[:, col(0)])
    for s in range(1, N_T):
        gate_value += nt(xs[s][...], wg[:, col(s)])
        up_value += nt(xs[s][...], wu[:, col(s)])
        grad_hidden += nt(gs[s][...], wd[:, col(s)])
    sigma = jax.nn.sigmoid(gate_value)
    silu = gate_value * sigma
    hidden = (silu * up_value).astype(BF)
    gate_rows = (grad_hidden * up_value * sigma * (1.0 + gate_value * (1.0 - sigma))).astype(BF)
    up_rows = (grad_hidden * silu).astype(BF)

    product = hidden.astype(F32) * grad_hidden
    high = product.astype(BF)
    low = (product - high.astype(F32)).astype(BF)
    ones = jnp.ones((8, product.shape[1]), BF)
    dots = nt(ones, high) + nt(ones, low)
    line = lax.broadcasted_iota(jnp.int32, (8, width), 0)
    dots = jnp.where(line < 4, dots[:, :width], dots[:, width:]).astype(BF)
    for d in range(N_T - 1, -1, -1):
        part[d, :rows] = nn(hidden, wd[:, col(d)]).astype(BF)
        part[d, rows:] = dots
        gpart[d] = (nn(gate_rows, wg[:, col(d)]) + nn(up_rows, wu[:, col(d)])).astype(BF)
    for s in range(N_T):
        gout[:, col(s)] = tn(gate_rows, xs[s][...]).astype(BF)
        uout[:, col(s)] = tn(up_rows, xs[s][...]).astype(BF)
        dout[:, col(s)] = tn(hidden, gs[s][...]).astype(BF)


def expert_work(meta, xs, gs, wg, wu, wd):
    rows, width = xs[0].shape
    vmem = pl.BlockSpec(memory_space=pltpu.VMEM)
    grad = jax.ShapeDtypeStruct(wg.shape, BF)
    return pl.pallas_call(
        expert_kernel,
        out_shape=(
            jax.ShapeDtypeStruct((N_T, rows + 8, width), BF),
            jax.ShapeDtypeStruct((N_T, rows, width), BF),
            grad, grad, grad,
        ),
        in_specs=[pl.BlockSpec(memory_space=pltpu.SMEM)] + [vmem] * (2 * N_T + 3),
        out_specs=(vmem,) * 5,
        name="expert",
    )(meta, *xs, *gs, wg, wu, wd)


def body(tokens, expert_ids, route_weights, w_gate, w_up, w_down, out_grad):
    experts = lax.axis_size("expert")
    tok_rows, choose = expert_ids.shape
    width = tokens.shape[1]
    cap = tok_rows * 8 // experts
    slots = experts * cap
    z = lax.axis_index("tensor")

    ids_t = expert_ids.T
    hit = ids_t[:, None, :] == jnp.arange(experts, dtype=jnp.int32)[None, :, None]
    named = jnp.any(hit, axis=0)
    weight_et = jnp.sum(jnp.where(hit, route_weights.T[:, None, :], 0.0), axis=0)
    earlier = jnp.arange(tok_rows)[:, None] < jnp.arange(tok_rows)[None, :]
    place = nn(named.astype(BF), earlier.astype(BF))
    chosen = named[:, None, :] & (
        place[:, None, :] == jnp.arange(cap, dtype=F32)[None, :, None]
    )
    pick = chosen.reshape(slots, tok_rows).astype(BF)
    pick_w = jnp.where(chosen, weight_et[:, None, :], 0.0)
    slot_w = jnp.sum(pick_w, axis=2).reshape(slots)
    pick_w = pick_w.reshape(slots, tok_rows)

    rows = nn(pick, tokens).astype(BF)
    grads = (slot_w[:, None] * nn(pick, out_grad)).astype(BF)
    sent = jnp.concatenate(
        [rows.reshape(experts, cap, width), grads.reshape(experts, cap, width)], axis=1
    )
    got = lax.all_to_all(sent, "expert", split_axis=0, concat_axis=0, tiled=True)
    x0 = got[:, :cap].reshape(slots, width)
    g0 = got[:, cap:].reshape(slots, width)

    xs, gs = gather_ring(x0, g0)
    meta = z.astype(jnp.int32).reshape(1)
    part, gpart, gate_term, up_term, down_term = expert_work(
        meta, xs, gs, w_gate[0], w_up[0], w_down[0]
    )

    p = reduce_ring(part, N_T // 2, N_T // 2 - 1)
    g = reduce_ring(gpart, N_T // 2 - 1, N_T // 2)
    back, grad_back = p[:slots], g
    dots = p[slots:]
    slot_dots = jnp.concatenate([dots[0], dots[4]]).reshape(experts, cap)

    def over_dp(term):
        other = lax.ppermute(term, "dp", [(0, 1), (1, 0)])
        return (term.astype(F32) + other.astype(F32)).astype(BF)[None]

    gate_grad, up_grad, down_grad = over_dp(gate_term), over_dp(up_term), over_dp(down_term)

    extra = jnp.pad(slot_dots[:, None, :], ((0, 0), (0, 7), (0, width - cap)))
    sent = jnp.concatenate(
        [back.reshape(experts, cap, width), grad_back.reshape(experts, cap, width), extra], axis=1
    )
    got = lax.all_to_all(sent, "expert", split_axis=0, concat_axis=0, tiled=True)
    home = got[:, :cap].reshape(slots, width)
    grad_home = got[:, cap : 2 * cap].reshape(slots, width)
    slot_dots = got[:, 2 * cap, :cap].astype(F32)

    layer = lax.dot_general(
        pick_w, home.astype(F32), (((0,), (0,)), ((), ())),
        precision=lax.Precision.HIGHEST, preferred_element_type=F32,
    )
    grad_tok = tn(pick, grad_home)
    dots_et = jnp.sum(jnp.where(chosen, slot_dots[:, :, None], 0.0), axis=1)
    dots_kt = jnp.sum(jnp.where(hit, dots_et[None], 0.0), axis=1)
    grad_w = dots_kt.T / route_weights
    return layer.astype(BF), grad_tok.astype(BF), grad_w, gate_grad, up_grad, down_grad


def solution(mesh):
    placed = (
        P(("dp", "expert"), "tensor"),
        P(("dp", "expert"), None),
        P(("dp", "expert"), None),
        P("expert", "tensor", None),
        P("expert", "tensor", None),
        P("expert", "tensor", None),
        P(("dp", "expert"), "tensor"),
    )
    return jax.shard_map(
        body,
        mesh=mesh,
        in_specs=placed,
        out_specs=(
            P(("dp", "expert"), "tensor"),
            P(("dp", "expert"), "tensor"),
            P(("dp", "expert"), None),
            P("expert", "tensor", None),
            P("expert", "tensor", None),
            P("expert", "tensor", None),
        ),
        check_vma=False,
    )
```

```python
import jax
import jax.numpy as jnp
from jax import lax
from jax.experimental import pallas as pl
from jax.experimental.pallas import tpu as pltpu
from jax.sharding import PartitionSpec as P


BF = jnp.bfloat16
F32 = jnp.float32
N_T = 8
CAP = 16
FIRST = (4, 5)
REST = (3, 6, 2, 7, 1, 0)


def nt(left, right):
    return lax.dot_general(left, right, (((1,), (1,)), ((), ())), preferred_element_type=F32)


def tn(left, right):
    return lax.dot_general(left, right, (((0,), (0,)), ((), ())), preferred_element_type=F32)


def nn(left, right):
    return lax.dot_general(left, right, (((1,), (0,)), ((), ())), preferred_element_type=F32)


def shift(x, by):
    return lax.ppermute(x, "tensor", [(i, (i + by) % N_T) for i in range(N_T)])


def gather_ring(x, g):
    xs, gs = [x] + [None] * (N_T - 1), [g] + [None] * (N_T - 1)
    half = N_T // 2
    for s in range(1, half + 1):
        xs[-s] = shift(xs[(1 - s) % N_T], 1)
        gs[-s if s < half else s] = shift(gs[(1 - s) % N_T], 1) if s < half else shift(gs[s - 1], -1)
        if s < half:
            xs[s] = shift(xs[s - 1], -1)
            gs[s] = shift(gs[s - 1], -1)
    return xs, gs


def reduce_ring(terms):
    half = N_T // 2
    up, down = terms[half], terms[N_T + 1 - half]
    for s in range(1, half + 1):
        up = shift(up, 1)
        if s < half:
            down = shift(down, -1)
            up = (up.astype(F32) + terms[half - s].astype(F32)).astype(BF)
            if s < half - 1:
                down = (down.astype(F32) + terms[N_T + s + 1 - half].astype(F32)).astype(BF)
    return terms[0], up, down


def iota(shape, dim):
    return lax.broadcasted_iota(jnp.int32, shape, dim)


def call(kernel, out_shape, scalars=0):
    vmem = pl.BlockSpec(memory_space=pltpu.VMEM)

    def run(*args):
        smem = [pl.BlockSpec(memory_space=pltpu.SMEM)] * scalars
        return pl.pallas_call(
            kernel,
            out_shape=out_shape,
            in_specs=smem + [vmem] * (len(args) - scalars),
            out_specs=jax.tree.map(lambda _: vmem, out_shape),
        )(*args)

    return run


def dispatch_kernel(ids, weights, tokens, grads, sent, pick_w):
    experts, twice, width = sent.shape
    cap = twice // 2
    tok_rows = tokens.shape[0]
    choose = ids.shape[0]
    owner = iota((experts, tok_rows), 0)
    named = jnp.zeros((experts, tok_rows), F32)
    weight_et = jnp.zeros((experts, tok_rows), F32)
    for k in range(choose):
        hit = ids[k : k + 1, :] == owner
        named = jnp.where(hit, 1.0, named)
        weight_et = jnp.where(hit, weights[k : k + 1, :], weight_et)
    square = (tok_rows, tok_rows)
    earlier = jnp.where(iota(square, 0) < iota(square, 1), 1.0, 0.0).astype(BF)
    place = jnp.where(named > 0.0, nn(named.astype(BF), earlier), -1.0)
    grid = (experts, cap, tok_rows)
    flat = (experts * cap, tok_rows)
    place = jnp.broadcast_to(place[:, None, :], grid).reshape(flat)
    weight = jnp.broadcast_to(weight_et[:, None, :], grid).reshape(flat)
    slot = (iota(flat, 0) & (cap - 1)).astype(F32)
    chosen = place == slot
    pick = jnp.where(chosen, 1.0, 0.0).astype(BF)
    weight = jnp.where(chosen, weight, 0.0)
    pick_w[...] = weight
    slot_w = jnp.sum(weight, axis=1, keepdims=True)
    rows = nn(pick, tokens[...]).astype(BF)
    scaled = (slot_w * nn(pick, grads[...])).astype(BF)
    sent[:, :cap, :] = rows.reshape(experts, cap, width)
    sent[:, cap:, :] = scaled.reshape(experts, cap, width)


def chunk_cols(meta, width):
    places = [(meta[0] + s) & (N_T - 1) for s in range(N_T)]
    return [pl.ds(pl.multiple_of(at * width, width), width) for at in places]


def side(parts):
    return jnp.concatenate(list(parts), axis=1)


def expert_kernel(meta, *refs):
    xs, gs, refs = refs[:N_T], refs[N_T : 2 * N_T], refs[2 * N_T :]
    wg, wu, wd = refs[:3]
    parts = refs[3:5]
    hidden_ref, gate_ref, up_ref, dots_ref = refs[5:]
    slots, width = xs[0].shape
    blocks = slots // CAP
    cols = chunk_cols(meta, width)

    x = side(r[...] for r in xs)
    gate_value = nt(x, side(wg[:, c] for c in cols))
    up_value = nt(x, side(wu[:, c] for c in cols))
    grad_hidden = nt(side(r[...] for r in gs), side(wd[:, c] for c in cols))
    sigma = jax.nn.sigmoid(gate_value)
    silu = gate_value * sigma
    hidden = (silu * up_value).astype(BF)
    gate_rows = (grad_hidden * up_value * sigma * (1.0 + gate_value * (1.0 - sigma))).astype(BF)
    up_rows = (grad_hidden * silu).astype(BF)
    hidden_ref[...] = hidden
    gate_ref[...] = gate_rows
    up_ref[...] = up_rows

    product = hidden.astype(F32) * grad_hidden
    high = product.astype(BF)
    low = (product - high.astype(F32)).astype(BF)
    ones = jnp.ones((8, product.shape[1]), BF)
    line = (nt(ones, high) + nt(ones, low))[0:1]
    wide, tall = (blocks, slots), (slots, width)
    mine = iota(wide, 1) // CAP == iota(wide, 0)
    spread = jnp.where(mine, line, 0.0).astype(BF)
    place = jnp.where((iota(tall, 0) & (CAP - 1)) == iota(tall, 1), 1.0, 0.0).astype(BF)
    dots = nn(spread, place).astype(BF)
    dots_ref[...] = dots
    for d, part in zip(FIRST, parts):
        write_part(part, hidden, gate_rows, up_rows, dots, wg, wu, wd, cols[d])


def write_part(out, hidden, gate_rows, up_rows, dots, wg, wu, wd, col):
    slots, width = hidden.shape[0], out.shape[1]
    grid = (slots // CAP, CAP, width)
    part = nn(hidden, wd[:, col]).astype(BF)
    gpart = (nn(gate_rows, wg[:, col]) + nn(up_rows, wu[:, col])).astype(BF)
    both = jnp.concatenate([part.reshape(grid), gpart.reshape(grid)], axis=1)
    out[: 2 * slots] = both.reshape(2 * slots, width)
    out[2 * slots :] = dots


def rest_kernel(meta, hidden, gate_rows, up_rows, dots, wg, wu, wd, *parts):
    cols = chunk_cols(meta, parts[0].shape[1])
    for d, part in zip(REST, parts):
        write_part(
            part, hidden[...], gate_rows[...], up_rows[...], dots[...], wg, wu, wd, cols[d]
        )


def grads_kernel(meta, *refs):
    xs, gs = refs[:N_T], refs[N_T : 2 * N_T]
    hidden, gate_rows, up_rows, out = refs[2 * N_T :]
    cols = chunk_cols(meta, xs[0].shape[1])
    hidden_t, gate_t, up_t = hidden[...].T, gate_rows[...].T, up_rows[...].T
    for s in range(N_T):
        out[0, :, cols[s]] = nn(gate_t, xs[s][...]).astype(BF)
        out[1, :, cols[s]] = nn(up_t, xs[s][...]).astype(BF)
        out[2, :, cols[s]] = nn(hidden_t, gs[s][...]).astype(BF)


def pack_kernel(own, up, down, sent):
    experts, _, width = sent.shape
    both = 2 * CAP
    rows = experts * both
    total = own[...].astype(F32) + up[...].astype(F32) + down[...].astype(F32)
    sent[:, :both, :] = total[:rows].astype(BF).reshape(experts, both, width)
    dots = jnp.broadcast_to(total[rows:][:, None, :], (experts, 8, width))
    sent[:, both:, :] = dots.astype(BF)


def combine_kernel(ids, weights, pick_ref, got, layer, grad_tok, grad_w):
    experts, _, width = got.shape
    slots, tok_rows = pick_ref.shape
    cap = slots // experts
    pick_w = pick_ref[...]
    pick = jnp.where(pick_w > 0.0, 1.0, 0.0).astype(BF)
    high = pick_w.astype(BF)
    rest = pick_w - high.astype(F32)
    mid = rest.astype(BF)
    low = (rest - mid.astype(F32)).astype(BF)
    home = got[:, :cap, :].reshape(slots, width)
    layer[...] = (tn(high, home) + tn(mid, home) + tn(low, home)).astype(BF)
    grad_tok[...] = tn(pick, got[:, cap : 2 * cap, :].reshape(slots, width)).astype(BF)
    dots = (0.125 * jnp.sum(got[:, 2 * cap :, :].astype(F32), axis=1)).astype(BF)
    line = (width, slots)
    spread = jnp.where((iota(line, 1) & (cap - 1)) == iota(line, 0), 1.0, 0.0).astype(BF)
    wide = (experts, slots)
    dots = jnp.where(iota(wide, 1) // cap == iota(wide, 0), nn(dots, spread), 0.0).astype(BF)
    dots_et = nn(dots, pick)
    owner = iota((experts, tok_rows), 0)
    for k in range(ids.shape[0]):
        mine = jnp.where(ids[k : k + 1, :] == owner, dots_et, 0.0)
        grad_w[k : k + 1, :] = jnp.sum(mine, axis=0, keepdims=True) / weights[k : k + 1, :]


def body(tokens, expert_ids, route_weights, w_gate, w_up, w_down, out_grad):
    experts = lax.axis_size("expert")
    tok_rows, choose = expert_ids.shape
    width = tokens.shape[1]
    cap = tok_rows * 8 // experts
    slots = experts * cap
    hid = w_gate.shape[1]
    z = lax.axis_index("tensor")
    meta = z.astype(jnp.int32).reshape(1)
    ids, weights = expert_ids.T, route_weights.T

    def shaped(shape, dtype=BF):
        return jax.ShapeDtypeStruct(shape, dtype)

    sent, pick_w = call(
        dispatch_kernel, (shaped((experts, 2 * cap, width)), shaped((slots, tok_rows), F32))
    )(ids, weights, tokens, out_grad)
    got = lax.all_to_all(sent, "expert", split_axis=0, concat_axis=0, tiled=True)
    x0 = got[:, :cap].reshape(slots, width)
    g0 = got[:, cap:].reshape(slots, width)
    xs, gs = gather_ring(x0, g0)

    tall = shaped((2 * slots + experts, width))
    w_args = (w_gate[0], w_up[0], w_down[0])
    made = call(
        expert_kernel,
        (tall,) * 2 + (shaped((slots, hid)),) * 3 + (shaped((experts, width)),),
        scalars=1,
    )(meta, *xs, *gs, *w_args)

    rest = call(rest_kernel, (tall,) * 6, scalars=1)(
        meta, *made[2:], *w_args
    )
    parts = dict(zip(FIRST + REST, made[:2] + rest))
    sums = reduce_ring(parts)
    sent = call(pack_kernel, shaped((experts, 2 * cap + 8, width)))(*sums)
    sent, held = lax.optimization_barrier((sent, made[2:5]))
    got = lax.all_to_all(sent, "expert", split_axis=0, concat_axis=0, tiled=True)
    terms = call(grads_kernel, shaped((3, hid, N_T * width)), scalars=1)(meta, *xs, *gs, *held)
    others = lax.ppermute(terms, "dp", [(0, 1), (1, 0)])
    w_grads = [(terms[i].astype(F32) + others[i].astype(F32)).astype(BF)[None] for i in range(3)]

    layer, grad_tok, grad_w = call(
        combine_kernel,
        (shaped((tok_rows, width)), shaped((tok_rows, width)), shaped((choose, tok_rows), F32)),
    )(ids, weights, pick_w, got)
    return layer, grad_tok, grad_w.T, *w_grads


def solution(mesh):
    placed = (
        P(("dp", "expert"), "tensor"),
        P(("dp", "expert"), None),
        P(("dp", "expert"), None),
        P("expert", "tensor", None),
        P("expert", "tensor", None),
        P("expert", "tensor", None),
        P(("dp", "expert"), "tensor"),
    )
    return jax.shard_map(
        body,
        mesh=mesh,
        in_specs=placed,
        out_specs=(
            P(("dp", "expert"), "tensor"),
            P(("dp", "expert"), "tensor"),
            P(("dp", "expert"), None),
            P("expert", "tensor", None),
            P("expert", "tensor", None),
            P("expert", "tensor", None),
        ),
        check_vma=False,
    )
```
